256 devices in a mesh: depth: 64 (over x, y_lo, z), height: 4 (over y_hi, core).
Axes of the slice: x: 4, y: 4 (y_hi: 2, y_lo: 2; y = y_hi * 2 + y_lo), z: 8, core: 2. Of those that a mesh axis runs over, the one named last changes fastest.
Arguments:
- queries: bfloat16 [14336, 512], P('depth', 'height'), may hold values from -6 to 6
- key_vectors: bfloat16 [14336, 512], P('depth', 'height'), may hold values from -6 to 6
- value_vectors: bfloat16 [14336, 512], P('depth', 'height'), may hold values from -6 to 6
- grad_conv: bfloat16 [128, 16, 56, 256], P('depth', 'height'), may hold values from -6 to 6
- conv_weight: bfloat16 [3, 3, 3, 256, 256], replicated, may hold values from -0.078125 to 0.078125
- dec_weight: bfloat16 [512, 8, 256], replicated, may hold values from -0.125 to 0.125
Outputs:
- grad_queries: bfloat16 [14336, 512], P('depth', 'height')
- grad_keys: bfloat16 [14336, 512], P('depth', 'height')
- grad_values: bfloat16 [14336, 512], P('depth', 'height')
The draws below stay inside these ranges and needn't reach their ends.
All inputs are finite; a program needn't handle non-finite values.
Results may differ from the reference program's by a relative error of at most 0.024.
Values may be sent and summed in bfloat16 or wider, within the bound.
No kernel may reach another device: no remote copies, remote signals or barrier semaphores. Data moves between devices by JAX's collectives and lax.ppermute only.
A program may use at most 128 MiB of HBM per device.

```python
import math
import jax
import jax.numpy as jnp
from jax import lax

C = 256
HEADS = 8
HSZ = 64
HT = 8
WT = 28
HD = 512
TOKENS = 14336
N_DEPTH = 64


def draw_queries(key, part):
    own_key = jax.random.fold_in(key, 11)
    drawn = jnp.clip(jax.random.normal(own_key, (TOKENS, HEADS * HSZ), jnp.float32), -6.0, 6.0)
    return drawn.astype(jnp.bfloat16)


def draw_key_vectors(key, part):
    own_key = jax.random.fold_in(key, 23)
    drawn = jnp.clip(jax.random.normal(own_key, (TOKENS, HEADS * HSZ), jnp.float32), -6.0, 6.0)
    return drawn.astype(jnp.bfloat16)


def draw_value_vectors(key, part):
    own_key = jax.random.fold_in(key, 31)
    column_key = jax.random.fold_in(key, 37)
    column_mean = jax.random.normal(column_key, (1, HEADS * HSZ), jnp.float32)
    noise = jax.random.normal(own_key, (TOKENS, HEADS * HSZ), jnp.float32)
    return jnp.clip(column_mean + noise, -6.0, 6.0).astype(jnp.bfloat16)


def levels(stream_key, extent, shards, least, high):
    gain = 1.0
    for position, shards_of in shards:
        heights = jax.random.uniform(jax.random.fold_in(jax.random.fold_in(stream_key, 6), position), (shards_of,), jnp.float32, least / len(shards), high / len(shards))
        gain = gain * jnp.repeat(jnp.exp(heights), extent[position] // shards_of).reshape((-1,) + (1,) * (len(extent) - 1 - position))
    return gain


def centred(key, extent, spread, most, cuts=(), held_as=jnp.bfloat16):
    factor_of = levels(key, extent, cuts, -0.22, 0.18) if cuts else 1.0
    array = jax.random.normal(key, extent, jnp.float32) * spread * factor_of
    return jnp.minimum(jnp.maximum(array, -most), most).astype(held_as)


def setup_inputs(seed: int = 0) -> dict:
    key_of = jax.random.split(jax.random.key(seed), 7)
    return {
        "queries": draw_queries(jax.random.fold_in(key_of[6], 71), 0),
        "key_vectors": draw_key_vectors(jax.random.fold_in(key_of[6], 71), 0),
        "value_vectors": draw_value_vectors(jax.random.fold_in(key_of[6], 71), 0),
        "grad_conv": centred(key_of[3], (2 * TOKENS // (HT * WT), 2 * HT, 2 * WT, C), 1.0, 6.0, ((0, 64), (1, 4))),
        "conv_weight": centred(key_of[4], (3, 3, 3, C, C), (27 * C) ** -0.5, 0.078125),
        "dec_weight": centred(key_of[5], (HD, 8, C), (8 * C) ** -0.5, 0.125),
    }


LOSS_SCALE = 64.0

def conv_grads(grad_conv, conv_weight):
    volume = grad_conv.astype(jnp.float32)
    padded = jnp.pad(volume, ((1, 1), (1, 1), (1, 1), (0, 0)))
    depth_len = volume.shape[0]
    rows_len = volume.shape[1]
    cols_len = volume.shape[2]
    kernel = conv_weight.astype(jnp.float32)
    summed = jnp.zeros(volume.shape, jnp.float32)
    for along_depth in range(3):
        for along_rows in range(3):
            for along_cols in range(3):
                window = padded[2 - along_depth:2 - along_depth + depth_len, 2 - along_rows:2 - along_rows + rows_len, 2 - along_cols:2 - along_cols + cols_len]
                summed = summed + jnp.einsum('dhwc,ec->dhwe', window, kernel[along_depth, along_rows, along_cols], precision=lax.Precision.HIGHEST)
    return (LOSS_SCALE * summed).astype(jnp.bfloat16)

def output_grads(voxel_grads, dec_weight):
    grouped = voxel_grads.reshape(N_DEPTH, 2, HT, 2, WT, 2, C)
    grouped = grouped.transpose(0, 2, 4, 1, 3, 5, 6).reshape(TOKENS, 8 * C)
    decoder = dec_weight.reshape(HEADS * HSZ, 8 * C)
    return jnp.dot(grouped, decoder.T, preferred_element_type=jnp.float32).astype(jnp.bfloat16)

def attention_grads(queries, key_vectors, value_vectors, out_grads):
    head_scale = 1.0 / math.sqrt(HSZ)
    query_all = queries.astype(jnp.float32).reshape(TOKENS, HEADS, HSZ)
    key_all = key_vectors.astype(jnp.float32).reshape(TOKENS, HEADS, HSZ)
    value_all = value_vectors.astype(jnp.float32).reshape(TOKENS, HEADS, HSZ)
    grad_all = out_grads.astype(jnp.float32).reshape(TOKENS, HEADS, HSZ)
    block_len = HT * WT

    def sweep(carried, block_index):
        key_acc, value_acc = carried
        row_start = (block_index * block_len).astype(jnp.int32)
        query_rows = lax.dynamic_slice_in_dim(query_all, row_start, block_len, 0)
        grad_block = lax.dynamic_slice_in_dim(grad_all, row_start, block_len, 0)
        logits = jnp.einsum('qhd,khd->hqk', query_rows, key_all) * head_scale
        row_max = lax.optimization_barrier(jnp.max(logits, axis=2, keepdims=True))
        log_norm = row_max + jnp.log(lax.optimization_barrier(jnp.sum(jnp.exp(logits - row_max), axis=2, keepdims=True)))
        softmax_rows = jnp.exp(logits - log_norm)
        slopes = jnp.einsum('qhd,khd->hqk', grad_block, value_all)
        delta_rows = lax.optimization_barrier(jnp.sum(softmax_rows * slopes, axis=2, keepdims=True))
        score_grads = lax.optimization_barrier((softmax_rows * (slopes - delta_rows)).astype(jnp.bfloat16)).astype(jnp.float32)
        prob_rows = lax.optimization_barrier(softmax_rows.astype(jnp.bfloat16)).astype(jnp.float32)
        query_part = jnp.einsum('hqk,khd->qhd', score_grads, key_all) * head_scale
        key_acc = key_acc + jnp.einsum('hqk,qhd->khd', score_grads, query_rows) * head_scale
        value_acc = value_acc + jnp.einsum('hqk,qhd->khd', prob_rows, grad_block)
        return ((key_acc, value_acc), query_part)
    start_acc = jnp.zeros((TOKENS, HEADS, HSZ), jnp.float32)
    final_accs, query_parts = lax.scan(sweep, (start_acc, start_acc), jnp.arange(N_DEPTH, dtype=jnp.int32))
    grad_queries = query_parts.reshape(TOKENS, HEADS * HSZ).astype(jnp.bfloat16)
    grad_keys = final_accs[0].reshape(TOKENS, HEADS * HSZ).astype(jnp.bfloat16)
    grad_values = final_accs[1].reshape(TOKENS, HEADS * HSZ).astype(jnp.bfloat16)
    return (grad_queries, grad_keys, grad_values)

def reference(queries, key_vectors, value_vectors, grad_conv, conv_weight, dec_weight):
    voxel_grads = conv_grads(grad_conv, conv_weight)
    out_grads = output_grads(voxel_grads, dec_weight)
    grad_queries, grad_keys, grad_values = attention_grads(queries, key_vectors, value_vectors, out_grads)
    return (grad_queries, grad_keys, grad_values)
```

```python
import math

import jax
import jax.numpy as jnp
from jax import lax
from jax.experimental import pallas as pl
from jax.experimental.pallas import tpu as pltpu
from jax.sharding import Mesh
from jax.sharding import PartitionSpec as P

HSZ = 64
LOSS_SCALE = 64.0
NEG_START = -1e30
HEAD_SCALE = 1.0 / math.sqrt(HSZ)
LOG2_SCALE = math.log2(math.e) / math.sqrt(HSZ)
KEY_AXES = ("x", "y")
QUERY_AXIS = "z"
DEPTH = ("x", "y", "z")
SPAN = 64
TILE = 256


def halo_pair(block, axis, dim):
    count = lax.axis_size(axis)
    forward = [(i, i + 1) for i in range(count - 1)]
    backward = [(target, source) for source, target in forward]
    last = lax.slice_in_dim(block, block.shape[dim] - 1, None, axis=dim)
    low = lax.ppermute(last, axis, forward)
    high = lax.ppermute(lax.slice_in_dim(block, 0, 1, axis=dim), axis, backward)
    return low, high


def product(left, right):
    return lax.dot_general(
        left, right, (((1,), (0,)), ((), ())), preferred_element_type=jnp.float32
    )


def product_t(left, right):
    return lax.dot_general(
        left, right, (((1,), (1,)), ((), ())), preferred_element_type=jnp.float32
    )


def conv_body(
    own_ref, before_ref, after_ref, above_ref, below_ref, w_ref, dec_ref, out_ref, x_ref, acc_ref, vox_ref, tok_ref
):
    step = pl.program_id(0)
    planes, rows, cols, channels = own_ref.shape

    @pl.when(step == 0)
    def _():
        for d in range(planes + 2):
            for r in range(rows + 2):
                if r == 0:
                    row = above_ref[d, 0]
                elif r == rows + 1:
                    row = below_ref[d, 0]
                elif d == 0:
                    row = before_ref[0, r - 1]
                elif d == planes + 1:
                    row = after_ref[0, r - 1]
                else:
                    row = own_ref[d - 1, r - 1]
                row = row.astype(jnp.float32)
                row = jnp.concatenate(
                    [row, jnp.zeros((SPAN - cols, channels), jnp.float32)], axis=0
                )
                x_ref[0, d, r] = pltpu.roll(row, SPAN - 1, 0).astype(jnp.bfloat16)
                x_ref[1, d, r] = row.astype(jnp.bfloat16)
                x_ref[2, d, r] = pltpu.roll(row, 1, 0).astype(jnp.bfloat16)
        acc_ref[...] = jnp.zeros_like(acc_ref)

    along_depth = step // 3
    along_rows = step % 3
    summed = acc_ref[...]
    for tap in range(3):
        window = x_ref[tap, pl.ds(2 - along_depth, planes), pl.ds(2 - along_rows, rows)]
        summed += product_t(window.reshape(planes * rows * SPAN, channels), w_ref[0, 0, tap])
    acc_ref[...] = summed

    @pl.when(step == 8)
    def _():
        voxels = (LOSS_SCALE * summed).astype(jnp.bfloat16).astype(jnp.float32)
        lanes = vox_ref.shape[2]
        for side in range(channels // lanes):
            vox_ref[side] = voxels[:, side * lanes : (side + 1) * lanes]
        half = SPAN // 2
        tokens = None
        for s in range(8):
            a, b, c = s // 4, s // 2 % 2, s % 2
            parts = []
            for h in range(rows // 2):
                at = pl.ds((a * rows + 2 * h + b) * SPAN + c, half, stride=2)
                sides = [vox_ref[side, at, :] for side in range(channels // lanes)]
                parts.append(jnp.concatenate(sides, axis=1))
            part = product_t(
                jnp.concatenate(parts, axis=0).astype(jnp.bfloat16),
                dec_ref[:, s * channels : (s + 1) * channels],
            )
            tokens = part if tokens is None else tokens + part
        for h in range(rows // 2):
            tok_ref[h * (cols // 2) : (h + 1) * (cols // 2), :] = tokens[
                h * half : h * half + cols // 2
            ]
        done = tok_ref[...].astype(jnp.bfloat16)
        copies, heights, _, width = out_ref.shape
        for place in range(copies):
            for height in range(heights):
                out_ref[place, height] = done[:, height * width : (height + 1) * width]


def conv_tokens(own, before, after, above, below, weight, decoder, copies, heights):
    planes, rows, cols, channels = own.shape
    tokens = planes // 2 * (rows // 2) * (cols // 2)
    features = decoder.shape[0]

    def whole(array):
        return pl.BlockSpec(array.shape, lambda t: (0,) * array.ndim)

    out_shape = (copies, heights, tokens, features // heights)
    return pl.pallas_call(
        conv_body,
        grid=(9,),
        in_specs=[
            whole(own),
            whole(before),
            whole(after),
            whole(above),
            whole(below),
            pl.BlockSpec((1, 1, 3, channels, channels), lambda t: (t // 3, t % 3, 0, 0, 0)),
            whole(decoder),
        ],
        out_specs=pl.BlockSpec(out_shape, lambda t: (0, 0, 0, 0)),
        out_shape=jax.ShapeDtypeStruct(out_shape, jnp.bfloat16),
        scratch_shapes=[
            pltpu.VMEM((3, planes + 2, rows + 2, SPAN, channels), jnp.bfloat16),
            pltpu.VMEM((planes * rows * SPAN, channels), jnp.float32),
            pltpu.VMEM((channels // 128, planes * rows * SPAN, 128), jnp.float32),
            pltpu.VMEM((tokens, features), jnp.float32),
        ],
        name="conv",
    )(own, before, after, above, below, weight, decoder)


def own_rows(turned, head):
    rows = lax.broadcasted_iota(jnp.int32, turned.shape, 0) // HSZ
    return jnp.where(rows == head, turned, jnp.zeros_like(turned))


def stats_body(kv_ref, q_ref, g_ref, out_ref, qt_ref, gt_ref, *, rows):
    width = q_ref.shape[1]
    qt = q_ref[...].T
    gt = g_ref[...].T
    qt_ref[...] = qt
    gt_ref[...] = gt
    wide = qt.shape[1]
    for head in range(width // HSZ):
        qh = own_rows(qt, head)
        gh = own_rows(gt, head)

        def step(i, carried):
            top, total, weighted = carried
            at = pl.multiple_of(i * rows, rows)
            logits = product(kv_ref[pl.ds(at, rows), :width], qh).reshape(rows // 8, 8, wide)
            slopes = product(kv_ref[pl.ds(at, rows), width:], gh).reshape(rows // 8, 8, wide)
            new_top = jnp.maximum(top, jnp.max(logits, axis=0))
            fade = jnp.exp2((top - new_top) * LOG2_SCALE)
            weights = jnp.exp2((logits - new_top[None]) * LOG2_SCALE)
            total = total * fade + jnp.sum(weights, axis=0)
            weighted = weighted * fade + jnp.sum(weights * slopes, axis=0)
            return new_top, total, weighted

        zero = jnp.zeros((8, wide), jnp.float32)
        start = (jnp.full((8, wide), NEG_START, jnp.float32), zero, zero)
        top, total, weighted = lax.fori_loop(0, kv_ref.shape[0] // rows, step, start, unroll=True)
        best = jnp.max(top, axis=0, keepdims=True)
        fade = jnp.exp2((top - best) * LOG2_SCALE)
        total = jnp.sum(total * fade, axis=0, keepdims=True)
        weighted = jnp.sum(weighted * fade, axis=0, keepdims=True)
        log_sum = best * LOG2_SCALE + jnp.log2(total)
        delta = weighted / total
        for place in range(out_ref.shape[0]):
            out_ref[place, 2 * head : 2 * head + 1, :] = log_sum
            out_ref[place, 2 * head + 1 : 2 * head + 2, :] = delta


def local_stats(both, queries, grads, copies):
    count, pair = both.shape
    query_count, width = queries.shape
    heads = width // HSZ
    tile = pl.BlockSpec((TILE, width), lambda i: (i, 0))
    turned = pl.BlockSpec((width, TILE), lambda i: (0, i))
    return pl.pallas_call(
        lambda *refs: stats_body(*refs, rows=128),
        grid=(query_count // TILE,),
        in_specs=[pl.BlockSpec((count, pair), lambda i: (0, 0)), tile, tile],
        out_specs=[
            pl.BlockSpec((copies, 2 * heads, TILE), lambda i: (0, 0, i)),
            turned,
            turned,
        ],
        out_shape=[
            jax.ShapeDtypeStruct((copies, 2 * heads, query_count), jnp.float32),
            jax.ShapeDtypeStruct((width, query_count), jnp.bfloat16),
            jax.ShapeDtypeStruct((width, query_count), jnp.bfloat16),
        ],
        name="stats",
    )(both, queries, grads)


def grads_body(
    kv_ref, q_ref, g_ref, qt_ref, gt_ref, part_ref, dkv_ref, dq_ref, p_ref, s_ref, acc_ref, st_ref
):
    block = pl.program_id(0)
    rows = kv_ref.shape[0]
    count, width = q_ref.shape

    @pl.when(block == 0)
    def _():
        for head in range(width // HSZ):
            logs = part_ref[:, 2 * head, :]
            best = jnp.max(logs, axis=0, keepdims=True)
            shares = jnp.exp2(logs - best)
            total = jnp.sum(shares, axis=0, keepdims=True)
            delta = jnp.sum(shares * part_ref[:, 2 * head + 1, :], axis=0, keepdims=True)
            st_ref[2 * head : 2 * head + 1, :] = best + jnp.log2(total)
            st_ref[2 * head + 1 : 2 * head + 2, :] = delta / total
        acc_ref[...] = jnp.zeros_like(acc_ref)

    keys = kv_ref[:, :width]
    values = kv_ref[:, width:]
    keys_t = keys.T
    head_of = lax.broadcasted_iota(jnp.int32, (rows, width), 1) // HSZ
    dks = []
    dvs = []
    for head in range(width // HSZ):
        mine = head_of == head
        head_keys = jnp.where(mine, keys, jnp.zeros_like(keys))
        head_values = jnp.where(mine, values, jnp.zeros_like(values))
        for i in range(count // TILE):
            at = slice(i * TILE, (i + 1) * TILE)
            logits = product(head_keys, qt_ref[:, at])
            slopes = product(head_values, gt_ref[:, at])
            probs = jnp.exp2(logits * LOG2_SCALE - st_ref[2 * head : 2 * head + 1, at])
            p_ref[head, :, at] = probs.astype(jnp.bfloat16)
            s_ref[head, :, at] = (probs * (slopes - st_ref[2 * head + 1 : 2 * head + 2, at])).astype(
                jnp.bfloat16
            )
        dvs.append(product(p_ref[head], g_ref[...]))
        dks.append(product(s_ref[head], q_ref[...]))
        span = slice(head * HSZ, (head + 1) * HSZ)
        acc_ref[span, :] += product(keys_t[span], s_ref[head])
    dk, dv = (dks[-1], dvs[-1])
    for head in range(len(dks) - 1):
        dk = jnp.where(head_of == head, dks[head], dk)
        dv = jnp.where(head_of == head, dvs[head], dv)
    dkv_ref[:, :width] = (dk * HEAD_SCALE).astype(jnp.bfloat16)
    dkv_ref[:, width:] = dv.astype(jnp.bfloat16)

    @pl.when(block == pl.num_programs(0) - 1)
    def _():
        dq_ref[...] = (acc_ref[...] * HEAD_SCALE).T.astype(jnp.bfloat16)


def local_grads(both, queries, grads, queries_t, grads_t, parts):
    count, pair = both.shape
    query_count, width = queries.shape
    heads = width // HSZ
    rows = 256
    block = pl.BlockSpec((rows, pair), lambda i: (i, 0))

    def whole(*shape):
        return pl.BlockSpec(shape, lambda i: (0,) * len(shape))

    return pl.pallas_call(
        grads_body,
        grid=(count // rows,),
        in_specs=[
            block,
            whole(query_count, width),
            whole(query_count, width),
            whole(width, query_count),
            whole(width, query_count),
            whole(*parts.shape),
        ],
        out_specs=[block, whole(query_count, width)],
        out_shape=[
            jax.ShapeDtypeStruct((count, pair), jnp.bfloat16),
            jax.ShapeDtypeStruct((query_count, width), jnp.bfloat16),
        ],
        scratch_shapes=[
            pltpu.VMEM((heads, rows, query_count), jnp.bfloat16),
            pltpu.VMEM((heads, rows, query_count), jnp.bfloat16),
            pltpu.VMEM((width, query_count), jnp.float32),
            pltpu.VMEM((2 * heads, query_count), jnp.float32),
        ],
        name="grads",
    )(both, queries, grads, queries_t, grads_t, parts)


def spread_to(array, axes):
    count = lax.axis_size(axes)
    copies = jnp.broadcast_to(array[None], (count,) + array.shape)
    return lax.all_to_all(copies, axes, 0, 0, tiled=True)


def body(queries, key_vectors, value_vectors, grad_conv, conv_weight, dec_weight):
    tokens, width = queries.shape
    heights = lax.axis_size("height")
    places = lax.axis_size(QUERY_AXIS)
    before, after = halo_pair(grad_conv, DEPTH, 0)
    padded = jnp.concatenate([before, grad_conv, after], axis=0)
    above, below = halo_pair(padded, "height", 1)
    both = spread_to(jnp.concatenate([key_vectors, value_vectors], axis=1), KEY_AXES)
    both = both.reshape(-1, 2 * width)
    every_query = spread_to(queries, QUERY_AXIS).reshape(-1, width)
    decoder = dec_weight.reshape(dec_weight.shape[0], -1)
    apart = conv_tokens(
        grad_conv, before, after, above, below, conv_weight, decoder, places, heights
    )
    apart = apart.reshape((places * heights,) + apart.shape[2:])
    every_grad = lax.all_to_all(apart, (QUERY_AXIS, "height"), 0, 0, tiled=True).reshape(-1, width)
    part, queries_t, grads_t = local_stats(both, every_query, every_grad, places)
    parts = lax.all_to_all(part, QUERY_AXIS, 0, 0, tiled=True)
    dkv, dq = local_grads(both, every_query, every_grad, queries_t, grads_t, parts)
    arrived = lax.all_to_all(dkv.reshape(-1, tokens, 2 * width), KEY_AXES, 0, 0, tiled=True)
    owned = jnp.sum(arrived.astype(jnp.float32), axis=0).astype(jnp.bfloat16)
    dq = lax.all_to_all(dq.reshape(-1, tokens, width), QUERY_AXIS, 0, 0, tiled=True)
    dq = jnp.sum(dq.astype(jnp.float32), axis=0).astype(jnp.bfloat16)
    return dq, owned[:, :width], owned[:, width:]


def solution(mesh):
    fine = Mesh(mesh.devices.reshape(4, 2, 8, 4), ("x", "y", "z", "height"))
    in_specs = (
        P(DEPTH, "height"),
        P(DEPTH, "height"),
        P(DEPTH, "height"),
        P(DEPTH, "height", None, None),
        P(),
        P(),
    )
    out_specs = (P(DEPTH, "height"), P(DEPTH, "height"), P(DEPTH, "height"))
    return jax.shard_map(body, mesh=fine, in_specs=in_specs, out_specs=out_specs, check_vma=False)
```

```python
import math

import jax
import jax.numpy as jnp
from jax import lax
from jax.experimental import pallas as pl
from jax.experimental.pallas import tpu as pltpu
from jax.sharding import Mesh
from jax.sharding import PartitionSpec as P

HSZ = 64
LOSS_SCALE = 64.0
NEG_START = -1e30
HEAD_SCALE = 1.0 / math.sqrt(HSZ)
LOG2_SCALE = math.log2(math.e) / math.sqrt(HSZ)
KEY_AXES = ("x", "y")
QUERY_AXIS = "z"
DEPTH = ("x", "y", "z")
SPAN = 64
TILE = 256


def halo_pair(block, axis, dim):
    count = lax.axis_size(axis)
    forward = [(i, i + 1) for i in range(count - 1)]
    backward = [(target, source) for source, target in forward]
    last = lax.slice_in_dim(block, block.shape[dim] - 1, None, axis=dim)
    low = lax.ppermute(last, axis, forward)
    high = lax.ppermute(lax.slice_in_dim(block, 0, 1, axis=dim), axis, backward)
    return low, high


def product(left, right):
    return lax.dot_general(
        left, right, (((1,), (0,)), ((), ())), preferred_element_type=jnp.float32
    )


def product_t(left, right):
    return lax.dot_general(
        left, right, (((1,), (1,)), ((), ())), preferred_element_type=jnp.float32
    )


def conv_body(
    own_ref, before_ref, after_ref, above_ref, below_ref, w_ref, dec_ref, out_ref, x_ref, acc_ref, vox_ref, tok_ref
):
    planes, rows, cols, channels = own_ref.shape
    for d in range(planes + 2):
        for r in range(rows + 2):
            if r == 0:
                row = above_ref[d, 0]
            elif r == rows + 1:
                row = below_ref[d, 0]
            elif d == 0:
                row = before_ref[0, r - 1]
            elif d == planes + 1:
                row = after_ref[0, r - 1]
            else:
                row = own_ref[d - 1, r - 1]
            x_ref[d, r, :cols] = row
            x_ref[d, r, cols:] = jnp.zeros((SPAN - cols, channels), jnp.bfloat16)

    for step in range(9):
        along_depth, along_rows = (step // 3, step % 3)
        window = x_ref[2 - along_depth : 2 - along_depth + planes, 2 - along_rows : 2 - along_rows + rows]
        window = window.reshape(planes * rows * SPAN, channels)
        for tap in range(3):
            part = product_t(window, w_ref[along_depth, along_rows, tap])
            if step == 0:
                acc_ref[tap] = part
            else:
                acc_ref[tap] += part

    ahead = pltpu.roll(acc_ref[0], planes * rows * SPAN - 1, 0)
    summed = acc_ref[1] + ahead + pltpu.roll(acc_ref[2], 1, 0)
    voxels = (LOSS_SCALE * summed).astype(jnp.bfloat16).astype(jnp.float32)
    lanes = vox_ref.shape[2]
    for side in range(channels // lanes):
        vox_ref[side] = voxels[:, side * lanes : (side + 1) * lanes]
    half = SPAN // 2
    tokens = None
    for s in range(8):
        a, b, c = s // 4, s // 2 % 2, s % 2
        parts = []
        for h in range(rows // 2):
            at = pl.ds((a * rows + 2 * h + b) * SPAN + c, half, stride=2)
            sides = [vox_ref[side, at, :] for side in range(channels // lanes)]
            parts.append(jnp.concatenate(sides, axis=1))
        part = product_t(
            jnp.concatenate(parts, axis=0).astype(jnp.bfloat16),
            dec_ref[:, s * channels : (s + 1) * channels],
        )
        tokens = part if tokens is None else tokens + part
    for h in range(rows // 2):
        tok_ref[h * (cols // 2) : (h + 1) * (cols // 2), :] = tokens[
            h * half : h * half + cols // 2
        ]
    done = tok_ref[...].astype(jnp.bfloat16)
    copies, heights, _, width = out_ref.shape
    for place in range(copies):
        for height in range(heights):
            out_ref[place, height] = done[:, height * width : (height + 1) * width]


def conv_tokens(own, before, after, above, below, weight, decoder, copies, heights):
    planes, rows, cols, channels = own.shape
    tokens = planes // 2 * (rows // 2) * (cols // 2)
    features = decoder.shape[0]

    in_vmem = pl.BlockSpec(memory_space=pltpu.VMEM)
    out_shape = (copies, heights, tokens, features // heights)
    return pl.pallas_call(
        conv_body,
        in_specs=[in_vmem] * 7,
        out_specs=in_vmem,
        out_shape=jax.ShapeDtypeStruct(out_shape, jnp.bfloat16),
        scratch_shapes=[
            pltpu.VMEM((planes + 2, rows + 2, SPAN, channels), jnp.bfloat16),
            pltpu.VMEM((3, planes * rows * SPAN, channels), jnp.float32),
            pltpu.VMEM((channels // 128, planes * rows * SPAN, 128), jnp.float32),
            pltpu.VMEM((tokens, features), jnp.float32),
        ],
        name="conv",
    )(own, before, after, above, below, weight, decoder)


def own_rows(turned, head):
    rows = lax.broadcasted_iota(jnp.int32, turned.shape, 0) // HSZ
    return jnp.where(rows == head, turned, jnp.zeros_like(turned))


def stats_body(kv_ref, q_ref, g_ref, out_ref, qt_ref, gt_ref, *, rows):
    shards, _, per_shard, width = kv_ref.shape
    qt = q_ref[...].T
    gt = g_ref[...].T
    qt_ref[...] = qt
    gt_ref[...] = gt
    wide = qt.shape[1]
    for head in range(width // HSZ):
        qh = own_rows(qt, head)
        gh = own_rows(gt, head)

        zero = jnp.zeros((8, wide), jnp.float32)
        top, total, weighted = (jnp.full((8, wide), NEG_START, jnp.float32), zero, zero)
        for at in range(0, shards * per_shard, rows):
            span = pl.ds(at % per_shard, rows)
            logits = product(kv_ref[at // per_shard, 0, span], qh).reshape(rows // 8, 8, wide)
            slopes = product(kv_ref[at // per_shard, 1, span], gh).reshape(rows // 8, 8, wide)
            new_top = jnp.maximum(top, jnp.max(logits, axis=0))
            fade = jnp.exp2((top - new_top) * LOG2_SCALE)
            weights = jnp.exp2((logits - new_top[None]) * LOG2_SCALE)
            total = total * fade + jnp.sum(weights, axis=0)
            weighted = weighted * fade + jnp.sum(weights * slopes, axis=0)
            top = new_top
        best = jnp.max(top, axis=0, keepdims=True)
        fade = jnp.exp2((top - best) * LOG2_SCALE)
        total = jnp.sum(total * fade, axis=0, keepdims=True)
        weighted = jnp.sum(weighted * fade, axis=0, keepdims=True)
        log_sum = best * LOG2_SCALE + jnp.log2(total)
        delta = weighted / total
        for place in range(out_ref.shape[0]):
            out_ref[place, 2 * head : 2 * head + 1, :] = log_sum
            out_ref[place, 2 * head + 1 : 2 * head + 2, :] = delta


def local_stats(both, queries, grads, copies):
    query_count, width = queries.shape
    heads = width // HSZ
    tile = pl.BlockSpec((TILE, width), lambda i: (i, 0))
    turned = pl.BlockSpec((width, TILE), lambda i: (0, i))
    return pl.pallas_call(
        lambda *refs: stats_body(*refs, rows=112),
        grid=(query_count // TILE,),
        in_specs=[pl.BlockSpec(both.shape, lambda i: (0, 0, 0, 0)), tile, tile],
        out_specs=[
            pl.BlockSpec((copies, 2 * heads, TILE), lambda i: (0, 0, i)),
            turned,
            turned,
        ],
        out_shape=[
            jax.ShapeDtypeStruct((copies, 2 * heads, query_count), jnp.float32),
            jax.ShapeDtypeStruct((width, query_count), jnp.bfloat16),
            jax.ShapeDtypeStruct((width, query_count), jnp.bfloat16),
        ],
        name="stats",
    )(both, queries, grads)


def grads_body(kv_ref, q_ref, g_ref, qt_ref, gt_ref, part_ref, *rest):
    dkv_refs, (dq_ref, p_ref, s_ref, acc_ref, st_ref) = (rest[:-5], rest[-5:])
    block = pl.program_id(0)
    rows = kv_ref.shape[2]
    count, width = q_ref.shape

    @pl.when(block == 0)
    def _():
        for head in range(width // HSZ):
            logs = part_ref[:, 2 * head, :]
            best = jnp.max(logs, axis=0, keepdims=True)
            shares = jnp.exp2(logs - best)
            total = jnp.sum(shares, axis=0, keepdims=True)
            delta = jnp.sum(shares * part_ref[:, 2 * head + 1, :], axis=0, keepdims=True)
            st_ref[2 * head : 2 * head + 1, :] = best + jnp.log2(total)
            st_ref[2 * head + 1 : 2 * head + 2, :] = delta / total
        acc_ref[...] = jnp.zeros_like(acc_ref)

    keys = kv_ref[0, 0]
    values = kv_ref[0, 1]
    keys_t = keys.T
    head_of = lax.broadcasted_iota(jnp.int32, (rows, width), 1) // HSZ
    dks = []
    dvs = []
    for head in range(width // HSZ):
        mine = head_of == head
        head_keys = jnp.where(mine, keys, jnp.zeros_like(keys))
        head_values = jnp.where(mine, values, jnp.zeros_like(values))
        for i in range(count // TILE):
            at = slice(i * TILE, (i + 1) * TILE)
            logits = product(head_keys, qt_ref[:, at])
            slopes = product(head_values, gt_ref[:, at])
            probs = jnp.exp2(logits * LOG2_SCALE - st_ref[2 * head : 2 * head + 1, at])
            p_ref[head, :, at] = probs.astype(jnp.bfloat16)
            s_ref[head, :, at] = (probs * (slopes - st_ref[2 * head + 1 : 2 * head + 2, at])).astype(
                jnp.bfloat16
            )
        dvs.append(product(p_ref[head], g_ref[...]))
        dks.append(product(s_ref[head], q_ref[...]))
        span = slice(head * HSZ, (head + 1) * HSZ)
        acc_ref[span, :] += product(keys_t[span], s_ref[head])
    dk, dv = (dks[-1], dvs[-1])
    for head in range(len(dks) - 1):
        dk = jnp.where(head_of == head, dks[head], dk)
        dv = jnp.where(head_of == head, dvs[head], dv)
    dk = (dk * HEAD_SCALE).astype(jnp.bfloat16)
    dv = dv.astype(jnp.bfloat16)
    for shard, dkv_ref in enumerate(dkv_refs):

        @pl.when(block == shard)
        def _(dkv_ref=dkv_ref):
            dkv_ref[0] = dk
            dkv_ref[1] = dv

    @pl.when(block == pl.num_programs(0) - 1)
    def _():
        dq_ref[...] = (acc_ref[...] * HEAD_SCALE).T.astype(jnp.bfloat16)


def local_grads(both, queries, grads, queries_t, grads_t, parts):
    shards, _, rows, width = both.shape
    query_count = queries.shape[0]
    heads = width // HSZ

    def whole(*shape):
        return pl.BlockSpec(shape, lambda i: (0,) * len(shape))

    return pl.pallas_call(
        grads_body,
        grid=(shards,),
        in_specs=[
            pl.BlockSpec((1, 2, rows, width), lambda i: (i, 0, 0, 0)),
            whole(query_count, width),
            whole(query_count, width),
            whole(width, query_count),
            whole(width, query_count),
            whole(*parts.shape),
        ],
        out_specs=[whole(2, rows, width)] * shards + [whole(query_count, width)],
        out_shape=[jax.ShapeDtypeStruct((2, rows, width), jnp.bfloat16)] * shards
        + [jax.ShapeDtypeStruct((query_count, width), jnp.bfloat16)],
        scratch_shapes=[
            pltpu.VMEM((heads, rows, query_count), jnp.bfloat16),
            pltpu.VMEM((heads, rows, query_count), jnp.bfloat16),
            pltpu.VMEM((width, query_count), jnp.float32),
            pltpu.VMEM((2 * heads, query_count), jnp.float32),
        ],
        name="grads",
    )(both, queries, grads, queries_t, grads_t, parts)


def spread_to(array, axes):
    count = lax.axis_size(axes)
    copies = jnp.broadcast_to(array[None], (count,) + array.shape)
    return lax.all_to_all(copies, axes, 0, 0, tiled=True)


def moved(array, x_shift, y_shift):
    nx, ny = lax.axis_size("x"), lax.axis_size("y")
    pairs = [
        (x * ny + y, (x + x_shift) % nx * ny + (y + y_shift) % ny)
        for x in range(nx)
        for y in range(ny)
    ]
    return lax.ppermute(array, KEY_AXES, pairs)


X_SHIFTS = (0, 1, 3, 2)


def gathered_keys(own):
    other = moved(own, 0, 1)
    pair = jnp.stack([own, other])
    left = moved(pair, 1, 0)
    right = moved(pair, 3, 0)
    far = [moved(left[0], 1, 0), moved(right[1], 3, 0)]
    return jnp.concatenate([pair, left, right, jnp.stack(far)], axis=0)


def returned_keys(partial):
    total = partial[0].astype(jnp.float32)
    for at in range(1, len(partial)):
        total += moved(partial[at], -X_SHIFTS[at // 2], at % 2).astype(jnp.float32)
    return total.astype(jnp.bfloat16)


def body(queries, key_vectors, value_vectors, grad_conv, conv_weight, dec_weight):
    tokens, width = queries.shape
    heights = lax.axis_size("height")
    places = lax.axis_size(QUERY_AXIS)
    before, after = halo_pair(grad_conv, DEPTH, 0)
    padded = jnp.concatenate([before, grad_conv, after], axis=0)
    above, below = halo_pair(padded, "height", 1)
    both = gathered_keys(jnp.stack([key_vectors, value_vectors]))
    every_query = spread_to(queries, QUERY_AXIS).reshape(-1, width)
    decoder = dec_weight.reshape(dec_weight.shape[0], -1)
    apart = conv_tokens(
        grad_conv, before, after, above, below, conv_weight, decoder, places, heights
    )
    apart = apart.reshape((places * heights,) + apart.shape[2:])
    every_grad = lax.all_to_all(apart, (QUERY_AXIS, "height"), 0, 0, tiled=True)
    every_grad = every_grad.reshape(-1, width)
    part, queries_t, grads_t = local_stats(both, every_query, every_grad, places)
    parts = lax.all_to_all(part, QUERY_AXIS, 0, 0, tiled=True)
    *dkv, dq = local_grads(both, every_query, every_grad, queries_t, grads_t, parts)
    dq = lax.all_to_all(dq.reshape(-1, tokens, width), QUERY_AXIS, 0, 0, tiled=True)
    owned = returned_keys(dkv)
    dq = jnp.sum(dq.astype(jnp.float32), axis=0).astype(jnp.bfloat16)
    return dq, owned[0], owned[1]


def solution(mesh):
    fine = Mesh(mesh.devices.reshape(4, 2, 8, 4), ("x", "y", "z", "height"))
    in_specs = (
        P(DEPTH, "height"),
        P(DEPTH, "height"),
        P(DEPTH, "height"),
        P(DEPTH, "height", None, None),
        P(),
        P(),
    )
    out_specs = (P(DEPTH, "height"), P(DEPTH, "height"), P(DEPTH, "height"))
    return jax.shard_map(body, mesh=fine, in_specs=in_specs, out_specs=out_specs, check_vma=False)
```

```python
import math

import jax
import jax.numpy as jnp
from jax import lax
from jax.experimental import pallas as pl
from jax.experimental.pallas import tpu as pltpu
from jax.sharding import Mesh
from jax.sharding import PartitionSpec as P

HSZ = 64
LOSS_SCALE = 64.0
NEG_START = -1e30
HEAD_SCALE = 1.0 / math.sqrt(HSZ)
LOG2_SCALE = math.log2(math.e) / math.sqrt(HSZ)
KEY_AXES = ("x", "y")
QUERY_AXIS = "z"
DEPTH = ("x", "y", "z")
SPAN = 64
TILE = 256
GROUP = 2


def halo_pair(block, axis, dim):
    count = lax.axis_size(axis)
    forward = [(i, i + 1) for i in range(count - 1)]
    backward = [(target, source) for source, target in forward]
    last = lax.slice_in_dim(block, block.shape[dim] - 1, None, axis=dim)
    low = lax.ppermute(last, axis, forward)
    high = lax.ppermute(lax.slice_in_dim(block, 0, 1, axis=dim), axis, backward)
    return low, high


def product(left, right):
    return lax.dot_general(
        left, right, (((1,), (0,)), ((), ())), preferred_element_type=jnp.float32
    )


def product_t(left, right):
    return lax.dot_general(
        left, right, (((1,), (1,)), ((), ())), preferred_element_type=jnp.float32
    )


def conv_body(
    own_ref, before_ref, after_ref, above_ref, below_ref, w_ref, dec_ref, out_ref, x_ref, acc_ref, vox_ref, tok_ref
):
    planes, rows, cols, channels = own_ref.shape
    for d in range(planes + 2):
        for r in range(rows + 2):
            if r == 0:
                row = above_ref[d, 0]
            elif r == rows + 1:
                row = below_ref[d, 0]
            elif d == 0:
                row = before_ref[0, r - 1]
            elif d == planes + 1:
                row = after_ref[0, r - 1]
            else:
                row = own_ref[d - 1, r - 1]
            x_ref[d, r, :cols] = row
            x_ref[d, r, cols:] = jnp.zeros((SPAN - cols, channels), jnp.bfloat16)

    for step in range(9):
        along_depth, along_rows = (step // 3, step % 3)
        window = x_ref[2 - along_depth : 2 - along_depth + planes, 2 - along_rows : 2 - along_rows + rows]
        window = window.reshape(planes * rows * SPAN, channels)
        for tap in range(3):
            part = product_t(window, w_ref[along_depth, along_rows, tap])
            if step == 0:
                acc_ref[tap] = part
            else:
                acc_ref[tap] += part

    ahead = pltpu.roll(acc_ref[0], planes * rows * SPAN - 1, 0)
    summed = acc_ref[1] + ahead + pltpu.roll(acc_ref[2], 1, 0)
    voxels = (LOSS_SCALE * summed).astype(jnp.bfloat16).astype(jnp.float32)
    lanes = vox_ref.shape[2]
    for side in range(channels // lanes):
        vox_ref[side] = voxels[:, side * lanes : (side + 1) * lanes]
    half = SPAN // 2
    tokens = None
    for s in range(8):
        a, b, c = s // 4, s // 2 % 2, s % 2
        parts = []
        for h in range(rows // 2):
            at = pl.ds((a * rows + 2 * h + b) * SPAN + c, half, stride=2)
            sides = [vox_ref[side, at, :] for side in range(channels // lanes)]
            parts.append(jnp.concatenate(sides, axis=1))
        part = product_t(
            jnp.concatenate(parts, axis=0).astype(jnp.bfloat16),
            dec_ref[:, s * channels : (s + 1) * channels],
        )
        tokens = part if tokens is None else tokens + part
    for h in range(rows // 2):
        tok_ref[h * (cols // 2) : (h + 1) * (cols // 2), :] = tokens[
            h * half : h * half + cols // 2
        ]
    done = tok_ref[...].astype(jnp.bfloat16)
    copies, heights, _, width = out_ref.shape
    for place in range(copies):
        for height in range(heights):
            out_ref[place, height] = done[:, height * width : (height + 1) * width]


def conv_tokens(own, before, after, above, below, weight, decoder, copies, heights):
    planes, rows, cols, channels = own.shape
    tokens = planes // 2 * (rows // 2) * (cols // 2)
    features = decoder.shape[0]

    in_vmem = pl.BlockSpec(memory_space=pltpu.VMEM)
    out_shape = (copies, heights, tokens, features // heights)
    return pl.pallas_call(
        conv_body,
        in_specs=[in_vmem] * 7,
        out_specs=in_vmem,
        out_shape=jax.ShapeDtypeStruct(out_shape, jnp.bfloat16),
        scratch_shapes=[
            pltpu.VMEM((planes + 2, rows + 2, SPAN, channels), jnp.bfloat16),
            pltpu.VMEM((3, planes * rows * SPAN, channels), jnp.float32),
            pltpu.VMEM((channels // 128, planes * rows * SPAN, 128), jnp.float32),
            pltpu.VMEM((tokens, features), jnp.float32),
        ],
        name="conv",
    )(own, before, after, above, below, weight, decoder)


def own_rows(turned, head):
    rows = lax.broadcasted_iota(jnp.int32, turned.shape, 0) // HSZ
    return jnp.where(rows == head, turned, jnp.zeros_like(turned))


def stats_body(kv_ref, place_ref, g_ref, *refs, rows):
    q_refs, (out_ref, q_ref, qt_ref, gt_ref) = (refs[:-4], refs[-4:])
    shards, _, per_shard, width = kv_ref.shape

    @pl.when(pl.program_id(0) == 0)
    def _():
        count = len(q_refs)
        for back, shard_ref in enumerate(q_refs):
            at = (place_ref[0] + (count - back)) % count
            tokens = shard_ref.shape[0]
            q_ref[pl.ds(pl.multiple_of(at * tokens, tokens), tokens), :] = shard_ref[...]

    qt = q_ref[pl.ds(pl.multiple_of(pl.program_id(0) * TILE, TILE), TILE), :].T
    gt = g_ref[...].T
    qt_ref[...] = qt
    gt_ref[...] = gt
    wide = qt.shape[1]
    for head in range(width // HSZ):
        qh = own_rows(qt, head)
        gh = own_rows(gt, head)

        zero = jnp.zeros((8, wide), jnp.float32)
        top, total, weighted = (jnp.full((8, wide), NEG_START, jnp.float32), zero, zero)
        for at in range(0, shards * per_shard, rows):
            span = pl.ds(at % per_shard, rows)
            logits = product(kv_ref[at // per_shard, 0, span], qh).reshape(rows // 8, 8, wide)
            slopes = product(kv_ref[at // per_shard, 1, span], gh).reshape(rows // 8, 8, wide)
            new_top = jnp.maximum(top, jnp.max(logits, axis=0))
            fade = jnp.exp2((top - new_top) * LOG2_SCALE)
            weights = jnp.exp2((logits - new_top[None]) * LOG2_SCALE)
            total = total * fade + jnp.sum(weights, axis=0)
            weighted = weighted * fade + jnp.sum(weights * slopes, axis=0)
            top = new_top
        best = jnp.max(top, axis=0, keepdims=True)
        fade = jnp.exp2((top - best) * LOG2_SCALE)
        total = jnp.sum(total * fade, axis=0, keepdims=True)
        weighted = jnp.sum(weighted * fade, axis=0, keepdims=True)
        log_sum = best * LOG2_SCALE + jnp.log2(total)
        delta = weighted / total
        for place in range(out_ref.shape[0]):
            out_ref[place, 2 * head : 2 * head + 1, :] = log_sum
            out_ref[place, 2 * head + 1 : 2 * head + 2, :] = delta


def local_stats(both, shards, grads, copies):
    query_count, width = grads.shape
    place = lax.axis_index(QUERY_AXIS).astype(jnp.int32).reshape(1)
    heads = width // HSZ
    tile = pl.BlockSpec((TILE, width), lambda i: (i, 0))
    turned = pl.BlockSpec((width, TILE), lambda i: (0, i))
    return pl.pallas_call(
        lambda *refs: stats_body(*refs, rows=112),
        grid=(query_count // TILE,),
        in_specs=[
            pl.BlockSpec(both.shape, lambda i: (0, 0, 0, 0)),
            pl.BlockSpec(memory_space=pltpu.SMEM),
            tile,
        ]
        + [pl.BlockSpec(shards[0].shape, lambda i: (0, 0))] * len(shards),
        out_specs=[
            pl.BlockSpec((copies, 2 * heads, TILE), lambda i: (0, 0, i)),
            pl.BlockSpec((query_count, width), lambda i: (0, 0)),
            turned,
            turned,
        ],
        out_shape=[
            jax.ShapeDtypeStruct((copies, 2 * heads, query_count), jnp.float32),
            jax.ShapeDtypeStruct((query_count, width), jnp.bfloat16),
            jax.ShapeDtypeStruct((width, query_count), jnp.bfloat16),
            jax.ShapeDtypeStruct((width, query_count), jnp.bfloat16),
        ],
        name="stats",
    )(both, place, grads, *shards)


def grads_body(kv_ref, q_ref, g_ref, qt_ref, gt_ref, part_ref, *rest):
    dkv_refs, (dq_ref, p_ref, s_ref, acc_ref, st_ref) = (rest[:-5], rest[-5:])
    block = pl.program_id(0)
    group, _, per_shard, _ = kv_ref.shape
    rows = group * per_shard
    count, width = q_ref.shape

    @pl.when(block == 0)
    def _():
        for head in range(width // HSZ):
            logs = part_ref[:, 2 * head, :]
            best = jnp.max(logs, axis=0, keepdims=True)
            shares = jnp.exp2(logs - best)
            total = jnp.sum(shares, axis=0, keepdims=True)
            delta = jnp.sum(shares * part_ref[:, 2 * head + 1, :], axis=0, keepdims=True)
            st_ref[2 * head : 2 * head + 1, :] = best + jnp.log2(total)
            st_ref[2 * head + 1 : 2 * head + 2, :] = delta / total
        acc_ref[...] = jnp.zeros_like(acc_ref)

    keys = kv_ref[:, 0].reshape(rows, width)
    values = kv_ref[:, 1].reshape(rows, width)
    keys_t = keys.T
    head_of = lax.broadcasted_iota(jnp.int32, (rows, width), 1) // HSZ
    dks = []
    dvs = []
    for head in range(width // HSZ):
        mine = head_of == head
        head_keys = jnp.where(mine, keys, jnp.zeros_like(keys))
        head_values = jnp.where(mine, values, jnp.zeros_like(values))
        for i in range(count // TILE):
            at = slice(i * TILE, (i + 1) * TILE)
            logits = product(head_keys, qt_ref[:, at])
            slopes = product(head_values, gt_ref[:, at])
            probs = jnp.exp2(logits * LOG2_SCALE - st_ref[2 * head : 2 * head + 1, at])
            p_ref[head, :, at] = probs.astype(jnp.bfloat16)
            s_ref[head, :, at] = (probs * (slopes - st_ref[2 * head + 1 : 2 * head + 2, at])).astype(
                jnp.bfloat16
            )
        dvs.append(product(p_ref[head], g_ref[...]))
        dks.append(product(s_ref[head], q_ref[...]))
        span = slice(head * HSZ, (head + 1) * HSZ)
        acc_ref[span, :] += product(keys_t[span], s_ref[head])
    dk, dv = (dks[-1], dvs[-1])
    for head in range(len(dks) - 1):
        dk = jnp.where(head_of == head, dks[head], dk)
        dv = jnp.where(head_of == head, dvs[head], dv)
    dk = (dk * HEAD_SCALE).astype(jnp.bfloat16)
    dv = dv.astype(jnp.bfloat16)
    for shard, dkv_ref in enumerate(dkv_refs):

        span = slice(shard % group * per_shard, (shard % group + 1) * per_shard)

        @pl.when(block == shard // group)
        def _(dkv_ref=dkv_ref, span=span):
            dkv_ref[0] = dk[span]
            dkv_ref[1] = dv[span]

    @pl.when(block == pl.num_programs(0) - 1)
    def _():
        dq_ref[...] = (acc_ref[...] * HEAD_SCALE).T.astype(jnp.bfloat16)


def local_grads(both, queries, grads, queries_t, grads_t, parts):
    shards, _, rows, width = both.shape
    query_count = queries.shape[0]
    heads = width // HSZ

    def whole(*shape):
        return pl.BlockSpec(shape, lambda i: (0,) * len(shape))

    return pl.pallas_call(
        grads_body,
        grid=(shards // GROUP,),
        in_specs=[
            pl.BlockSpec((GROUP, 2, rows, width), lambda i: (i, 0, 0, 0)),
            whole(query_count, width),
            whole(query_count, width),
            whole(width, query_count),
            whole(width, query_count),
            whole(*parts.shape),
        ],
        out_specs=[whole(2, rows, width)] * shards + [whole(query_count, width)],
        out_shape=[jax.ShapeDtypeStruct((2, rows, width), jnp.bfloat16)] * shards
        + [jax.ShapeDtypeStruct((query_count, width), jnp.bfloat16)],
        scratch_shapes=[
            pltpu.VMEM((heads, GROUP * rows, query_count), jnp.bfloat16),
            pltpu.VMEM((heads, GROUP * rows, query_count), jnp.bfloat16),
            pltpu.VMEM((width, query_count), jnp.float32),
            pltpu.VMEM((2 * heads, query_count), jnp.float32),
        ],
        name="grads",
    )(both, queries, grads, queries_t, grads_t, parts)


def ring_step(array, shift):
    count = lax.axis_size(QUERY_AXIS)
    return lax.ppermute(array, QUERY_AXIS, [(i, (i + shift) % count) for i in range(count)])


def gathered_queries(own):
    up, down = [ring_step(own, 1)], [ring_step(own, -1)]
    up.append(ring_step(up[-1], 1))
    down.append(ring_step(down[-1], -1))
    up.append(ring_step(up[-1], 1))
    down.append(ring_step(down[-1], -1))
    up.append(ring_step(up[-1], 1))
    return [own] + up + down[::-1]


def moved(array, x_shift, y_shift):
    nx, ny = lax.axis_size("x"), lax.axis_size("y")
    pairs = [
        (x * ny + y, (x + x_shift) % nx * ny + (y + y_shift) % ny)
        for x in range(nx)
        for y in range(ny)
    ]
    return lax.ppermute(array, KEY_AXES, pairs)


X_SHIFTS = (0, 1, 3, 2)


def gathered_keys(own):
    other = moved(own, 0, 1)
    pair = jnp.stack([own, other])
    left = moved(pair, 1, 0)
    right = moved(pair, 3, 0)
    far = [moved(left[0], 1, 0), moved(right[1], 3, 0)]
    return jnp.concatenate([pair, left, right, jnp.stack(far)], axis=0)


def returned_keys(partial):
    total = partial[0].astype(jnp.float32)
    for at in range(1, len(partial)):
        total += moved(partial[at], -X_SHIFTS[at // 2], at % 2).astype(jnp.float32)
    return total.astype(jnp.bfloat16)


def body(queries, key_vectors, value_vectors, grad_conv, conv_weight, dec_weight):
    tokens, width = queries.shape
    heights = lax.axis_size("height")
    places = lax.axis_size(QUERY_AXIS)
    before, after = halo_pair(grad_conv, DEPTH, 0)
    padded = jnp.concatenate([before, grad_conv, after], axis=0)
    above, below = halo_pair(padded, "height", 1)
    both = gathered_keys(jnp.stack([key_vectors, value_vectors]))
    query_shards = gathered_queries(queries)
    decoder = dec_weight.reshape(dec_weight.shape[0], -1)
    apart = conv_tokens(
        grad_conv, before, after, above, below, conv_weight, decoder, places, heights
    )
    apart = apart.reshape((places * heights,) + apart.shape[2:])
    every_grad = lax.all_to_all(apart, (QUERY_AXIS, "height"), 0, 0, tiled=True)
    every_grad = every_grad.reshape(-1, width)
    part, every_query, queries_t, grads_t = local_stats(both, query_shards, every_grad, places)
    parts = lax.all_to_all(part, QUERY_AXIS, 0, 0, tiled=True)
    *dkv, dq = local_grads(both, every_query, every_grad, queries_t, grads_t, parts)
    dq = lax.all_to_all(dq.reshape(-1, tokens, width), QUERY_AXIS, 0, 0, tiled=True)
    owned = returned_keys(dkv)
    dq = jnp.sum(dq.astype(jnp.float32), axis=0).astype(jnp.bfloat16)
    return dq, owned[0], owned[1]


def solution(mesh):
    fine = Mesh(mesh.devices.reshape(4, 2, 8, 4), ("x", "y", "z", "height"))
    in_specs = (
        P(DEPTH, "height"),
        P(DEPTH, "height"),
        P(DEPTH, "height"),
        P(DEPTH, "height", None, None),
        P(),
        P(),
    )
    out_specs = (P(DEPTH, "height"), P(DEPTH, "height"), P(DEPTH, "height"))
    return jax.shard_map(body, mesh=fine, in_specs=in_specs, out_specs=out_specs, check_vma=False)
```

```python
import math

import jax
import jax.numpy as jnp
from jax import lax
from jax.experimental import pallas as pl
from jax.experimental.pallas import tpu as pltpu
from jax.sharding import Mesh
from jax.sharding import PartitionSpec as P

HSZ = 64
LOSS_SCALE = 64.0
NEG_START = -1e30
HEAD_SCALE = 1.0 / math.sqrt(HSZ)
LOG2_SCALE = math.log2(math.e) / math.sqrt(HSZ)
KEY_AXES = ("x", "y")
QUERY_AXIS = "z"
DEPTH = ("x", "y", "z")
SPAN = 64
TILE = 256
GROUP = 2


def halo_pair(block, axis, dim):
    count = lax.axis_size(axis)
    forward = [(i, i + 1) for i in range(count - 1)]
    backward = [(target, source) for source, target in forward]
    last = lax.slice_in_dim(block, block.shape[dim] - 1, None, axis=dim)
    low = lax.ppermute(last, axis, forward)
    high = lax.ppermute(lax.slice_in_dim(block, 0, 1, axis=dim), axis, backward)
    return low, high


def product(left, right):
    return lax.dot_general(
        left, right, (((1,), (0,)), ((), ())), preferred_element_type=jnp.float32
    )


def product_t(left, right):
    return lax.dot_general(
        left, right, (((1,), (1,)), ((), ())), preferred_element_type=jnp.float32
    )


def conv_body(
    own_ref, before_ref, after_ref, above_ref, below_ref, w_ref, dec_ref, out_ref, x_ref, acc_ref, vox_ref, tok_ref
):
    planes, rows, cols, channels = own_ref.shape
    for d in range(planes + 2):
        for r in range(rows + 2):
            if r == 0:
                row = above_ref[d, 0]
            elif r == rows + 1:
                row = below_ref[d, 0]
            elif d == 0:
                row = before_ref[0, r - 1]
            elif d == planes + 1:
                row = after_ref[0, r - 1]
            else:
                row = own_ref[d - 1, r - 1]
            x_ref[d, r, :cols] = row
            x_ref[d, r, cols:] = jnp.zeros((SPAN - cols, channels), jnp.bfloat16)

    for step in range(9):
        along_depth, along_rows = (step // 3, step % 3)
        window = x_ref[2 - along_depth : 2 - along_depth + planes, 2 - along_rows : 2 - along_rows + rows]
        window = window.reshape(planes * rows * SPAN, channels)
        for tap in range(3):
            part = product_t(window, w_ref[along_depth, along_rows, tap])
            if step == 0:
                acc_ref[tap] = part
            else:
                acc_ref[tap] += part

    ahead = pltpu.roll(acc_ref[0], planes * rows * SPAN - 1, 0)
    summed = acc_ref[1] + ahead + pltpu.roll(acc_ref[2], 1, 0)
    voxels = (LOSS_SCALE * summed).astype(jnp.bfloat16).astype(jnp.float32)
    lanes = vox_ref.shape[2]
    for side in range(channels // lanes):
        vox_ref[side] = voxels[:, side * lanes : (side + 1) * lanes]
    half = SPAN // 2
    tokens = None
    for s in range(8):
        a, b, c = s // 4, s // 2 % 2, s % 2
        parts = []
        for h in range(rows // 2):
            at = pl.ds((a * rows + 2 * h + b) * SPAN + c, half, stride=2)
            sides = [vox_ref[side, at, :] for side in range(channels // lanes)]
            parts.append(jnp.concatenate(sides, axis=1))
        part = product_t(
            jnp.concatenate(parts, axis=0).astype(jnp.bfloat16),
            dec_ref[:, s * channels : (s + 1) * channels],
        )
        tokens = part if tokens is None else tokens + part
    for h in range(rows // 2):
        tok_ref[h * (cols // 2) : (h + 1) * (cols // 2), :] = tokens[
            h * half : h * half + cols // 2
        ]
    done = tok_ref[...].astype(jnp.bfloat16)
    copies, heights, _, width = out_ref.shape
    for place in range(copies):
        for height in range(heights):
            out_ref[place, height] = done[:, height * width : (height + 1) * width]


def conv_tokens(own, before, after, above, below, weight, decoder, copies, heights):
    planes, rows, cols, channels = own.shape
    tokens = planes // 2 * (rows // 2) * (cols // 2)
    features = decoder.shape[0]

    in_vmem = pl.BlockSpec(memory_space=pltpu.VMEM)
    out_shape = (copies, heights, tokens, features // heights)
    return pl.pallas_call(
        conv_body,
        in_specs=[in_vmem] * 7,
        out_specs=in_vmem,
        out_shape=jax.ShapeDtypeStruct(out_shape, jnp.bfloat16),
        scratch_shapes=[
            pltpu.VMEM((planes + 2, rows + 2, SPAN, channels), jnp.bfloat16),
            pltpu.VMEM((3, planes * rows * SPAN, channels), jnp.float32),
            pltpu.VMEM((channels // 128, planes * rows * SPAN, 128), jnp.float32),
            pltpu.VMEM((tokens, features), jnp.float32),
        ],
        name="conv",
    )(own, before, after, above, below, weight, decoder)


def own_rows(turned, head):
    rows = lax.broadcasted_iota(jnp.int32, turned.shape, 0) // HSZ
    return jnp.where(rows == head, turned, jnp.zeros_like(turned))


def stats_body(kv_ref, q_ref, g_ref, out_ref, qt_ref, gt_ref, *, rows):
    shards, _, per_shard, width = kv_ref.shape
    qt = q_ref[...].T
    gt = g_ref[...].T
    qt_ref[...] = qt
    gt_ref[...] = gt
    wide = qt.shape[1]
    for head in range(width // HSZ):
        qh = own_rows(qt, head)
        gh = own_rows(gt, head)

        zero = jnp.zeros((8, wide), jnp.float32)
        top, total, weighted = (jnp.full((8, wide), NEG_START, jnp.float32), zero, zero)
        for at in range(0, shards * per_shard, rows):
            span = pl.ds(at % per_shard, rows)
            logits = product(kv_ref[at // per_shard, 0, span], qh).reshape(rows // 8, 8, wide)
            slopes = product(kv_ref[at // per_shard, 1, span], gh).reshape(rows // 8, 8, wide)
            new_top = jnp.maximum(top, jnp.max(logits, axis=0))
            fade = jnp.exp2((top - new_top) * LOG2_SCALE)
            weights = jnp.exp2((logits - new_top[None]) * LOG2_SCALE)
            total = total * fade + jnp.sum(weights, axis=0)
            weighted = weighted * fade + jnp.sum(weights * slopes, axis=0)
            top = new_top
        best = jnp.max(top, axis=0, keepdims=True)
        fade = jnp.exp2((top - best) * LOG2_SCALE)
        total = jnp.sum(total * fade, axis=0, keepdims=True)
        weighted = jnp.sum(weighted * fade, axis=0, keepdims=True)
        log_sum = best * LOG2_SCALE + jnp.log2(total)
        delta = weighted / total
        for place in range(out_ref.shape[0]):
            out_ref[place, 2 * head : 2 * head + 1, :] = log_sum
            out_ref[place, 2 * head + 1 : 2 * head + 2, :] = delta


def local_stats(both, queries, grads, copies):
    query_count, width = queries.shape
    heads = width // HSZ
    tile = pl.BlockSpec((TILE, width), lambda i: (i, 0))
    turned = pl.BlockSpec((width, TILE), lambda i: (0, i))
    return pl.pallas_call(
        lambda *refs: stats_body(*refs, rows=112),
        grid=(query_count // TILE,),
        in_specs=[pl.BlockSpec(both.shape, lambda i: (0, 0, 0, 0)), tile, tile],
        out_specs=[
            pl.BlockSpec((copies, 2 * heads, TILE), lambda i: (0, 0, i)),
            turned,
            turned,
        ],
        out_shape=[
            jax.ShapeDtypeStruct((copies, 2 * heads, query_count), jnp.float32),
            jax.ShapeDtypeStruct((width, query_count), jnp.bfloat16),
            jax.ShapeDtypeStruct((width, query_count), jnp.bfloat16),
        ],
        name="stats",
    )(both, queries, grads)


def grads_body(kv_ref, q_ref, g_ref, qt_ref, gt_ref, part_ref, *rest):
    dkv_refs, (dq_ref, p_ref, s_ref, acc_ref, st_ref) = (rest[:-5], rest[-5:])
    block = pl.program_id(0)
    group, _, per_shard, _ = kv_ref.shape
    rows = group * per_shard
    count, width = q_ref.shape

    @pl.when(block == 0)
    def _():
        for head in range(width // HSZ):
            logs = part_ref[:, 2 * head, :]
            best = jnp.max(logs, axis=0, keepdims=True)
            shares = jnp.exp2(logs - best)
            total = jnp.sum(shares, axis=0, keepdims=True)
            delta = jnp.sum(shares * part_ref[:, 2 * head + 1, :], axis=0, keepdims=True)
            st_ref[2 * head : 2 * head + 1, :] = best + jnp.log2(total)
            st_ref[2 * head + 1 : 2 * head + 2, :] = delta / total
        acc_ref[...] = jnp.zeros_like(acc_ref)

    keys = kv_ref[:, 0].reshape(rows, width)
    values = kv_ref[:, 1].reshape(rows, width)
    keys_t = keys.T
    head_of = lax.broadcasted_iota(jnp.int32, (rows, width), 1) // HSZ
    dks = []
    dvs = []
    for head in range(width // HSZ):
        mine = head_of == head
        head_keys = jnp.where(mine, keys, jnp.zeros_like(keys))
        head_values = jnp.where(mine, values, jnp.zeros_like(values))
        for i in range(count // TILE):
            at = slice(i * TILE, (i + 1) * TILE)
            logits = product(head_keys, qt_ref[:, at])
            slopes = product(head_values, gt_ref[:, at])
            probs = jnp.exp2(logits * LOG2_SCALE - st_ref[2 * head : 2 * head + 1, at])
            p_ref[head, :, at] = probs.astype(jnp.bfloat16)
            s_ref[head, :, at] = (probs * (slopes - st_ref[2 * head + 1 : 2 * head + 2, at])).astype(
                jnp.bfloat16
            )
        dvs.append(product(p_ref[head], g_ref[...]))
        dks.append(product(s_ref[head], q_ref[...]))
        span = slice(head * HSZ, (head + 1) * HSZ)
        acc_ref[span, :] += product(keys_t[span], s_ref[head])
    dk, dv = (dks[-1], dvs[-1])
    for head in range(len(dks) - 1):
        dk = jnp.where(head_of == head, dks[head], dk)
        dv = jnp.where(head_of == head, dvs[head], dv)
    dk = (dk * HEAD_SCALE).astype(jnp.bfloat16)
    dv = dv.astype(jnp.bfloat16)
    for shard, dkv_ref in enumerate(dkv_refs):

        span = slice(shard % group * per_shard, (shard % group + 1) * per_shard)

        @pl.when(block == shard // group)
        def _(dkv_ref=dkv_ref, span=span):
            dkv_ref[0] = dk[span]
            dkv_ref[1] = dv[span]

    @pl.when(block == pl.num_programs(0) - 1)
    def _():
        dq_ref[...] = (acc_ref[...] * HEAD_SCALE).T.astype(jnp.bfloat16)


def local_grads(both, queries, grads, queries_t, grads_t, parts):
    shards, _, rows, width = both.shape
    query_count = queries.shape[0]
    heads = width // HSZ

    def whole(*shape):
        return pl.BlockSpec(shape, lambda i: (0,) * len(shape))

    return pl.pallas_call(
        grads_body,
        grid=(shards // GROUP,),
        in_specs=[
            pl.BlockSpec((GROUP, 2, rows, width), lambda i: (i, 0, 0, 0)),
            whole(query_count, width),
            whole(query_count, width),
            whole(width, query_count),
            whole(width, query_count),
            whole(*parts.shape),
        ],
        out_specs=[whole(2, rows, width)] * shards + [whole(query_count, width)],
        out_shape=[jax.ShapeDtypeStruct((2, rows, width), jnp.bfloat16)] * shards
        + [jax.ShapeDtypeStruct((query_count, width), jnp.bfloat16)],
        scratch_shapes=[
            pltpu.VMEM((heads, GROUP * rows, query_count), jnp.bfloat16),
            pltpu.VMEM((heads, GROUP * rows, query_count), jnp.bfloat16),
            pltpu.VMEM((width, query_count), jnp.float32),
            pltpu.VMEM((2 * heads, query_count), jnp.float32),
        ],
        name="grads",
    )(both, queries, grads, queries_t, grads_t, parts)


def spread_to(array, axes):
    count = lax.axis_size(axes)
    copies = jnp.broadcast_to(array[None], (count,) + array.shape)
    return lax.all_to_all(copies, axes, 0, 0, tiled=True)


def moved(array, x_shift, y_shift):
    nx, ny = lax.axis_size("x"), lax.axis_size("y")
    pairs = [
        (x * ny + y, (x + x_shift) % nx * ny + (y + y_shift) % ny)
        for x in range(nx)
        for y in range(ny)
    ]
    return lax.ppermute(array, KEY_AXES, pairs)


X_SHIFTS = (0, 1, 3, 2)


def gathered_keys(own):
    other = moved(own, 0, 1)
    pair = jnp.stack([own, other])
    left = moved(pair, 1, 0)
    right = moved(pair, 3, 0)
    far = [moved(left[0], 1, 0), moved(right[1], 3, 0)]
    return jnp.concatenate([pair, left, right, jnp.stack(far)], axis=0)


def returned_keys(partial):
    total = partial[0].astype(jnp.float32)
    for at in range(1, len(partial)):
        total += moved(partial[at], -X_SHIFTS[at // 2], at % 2).astype(jnp.float32)
    return total.astype(jnp.bfloat16)


def body(queries, key_vectors, value_vectors, grad_conv, conv_weight, dec_weight):
    tokens, width = queries.shape
    heights = lax.axis_size("height")
    places = lax.axis_size(QUERY_AXIS)
    before, after = halo_pair(grad_conv, DEPTH, 0)
    padded = jnp.concatenate([before, grad_conv, after], axis=0)
    above, below = halo_pair(padded, "height", 1)
    both = gathered_keys(jnp.stack([key_vectors, value_vectors]))
    every_query = spread_to(queries, QUERY_AXIS).reshape(-1, width)
    decoder = dec_weight.reshape(dec_weight.shape[0], -1)
    apart = conv_tokens(
        grad_conv, before, after, above, below, conv_weight, decoder, places, heights
    )
    apart = apart.reshape((places * heights,) + apart.shape[2:])
    every_grad = lax.all_to_all(apart, (QUERY_AXIS, "height"), 0, 0, tiled=True)
    every_grad = every_grad.reshape(-1, width)
    part, queries_t, grads_t = local_stats(both, every_query, every_grad, places)
    parts = lax.all_to_all(part, QUERY_AXIS, 0, 0, tiled=True)
    *dkv, dq = local_grads(both, every_query, every_grad, queries_t, grads_t, parts)
    dq = lax.all_to_all(dq.reshape(-1, tokens, width), QUERY_AXIS, 0, 0, tiled=True)
    owned = returned_keys(dkv)
    dq = jnp.sum(dq.astype(jnp.float32), axis=0).astype(jnp.bfloat16)
    return dq, owned[0], owned[1]


def solution(mesh):
    fine = Mesh(mesh.devices.reshape(4, 2, 8, 4), ("x", "y", "z", "height"))
    in_specs = (
        P(DEPTH, "height"),
        P(DEPTH, "height"),
        P(DEPTH, "height"),
        P(DEPTH, "height", None, None),
        P(),
        P(),
    )
    out_specs = (P(DEPTH, "height"), P(DEPTH, "height"), P(DEPTH, "height"))
    return jax.shard_map(body, mesh=fine, in_specs=in_specs, out_specs=out_specs, check_vma=False)
```
